32 devices in a mesh: dp: 4 (over z), row: 4 (over x, core), col: 2 (over y).
Axes of the slice: x: 2, y: 2, z: 4, core: 2. Of those that a mesh axis runs over, the one named last changes fastest.
Arguments:
- hidden_in: bfloat16 [8192, 1536], P(('dp', 'row'), 'col'), may hold values from -6 to 6
- attn_gain: float32 [1536], P('col'), may hold values from 0.5 to 1.5
- w_query: bfloat16 [1536, 1536], P('col', 'row'), may hold values from -0.15625 to 0.15625
- w_key: bfloat16 [1536, 768], P('col', 'row'), may hold values from -0.15625 to 0.15625
- w_value: bfloat16 [1536, 768], P('col', 'row'), may hold values from -0.15625 to 0.15625
- w_output: bfloat16 [1536, 1536], P('row', 'col'), may hold values from -1.25 to 1.25
- mlp_gain: float32 [1536], P('col'), may hold values from 0.5 to 1.5
- w_gate: bfloat16 [1536, 4096], P('col', 'row'), may hold values from -0.15625 to 0.15625
- w_up: bfloat16 [1536, 4096], P('col', 'row'), may hold values from -0.15625 to 0.15625
- w_down: bfloat16 [4096, 1536], P('row', 'col'), may hold values from -0.09375 to 0.09375
- grad_out: bfloat16 [8192, 1536], P(('dp', 'row'), 'col'), may hold values from -6 to 6
Outputs:
- layer_out: bfloat16 [8192, 1536], P(('dp', 'row'), 'col')
- grad_in: float32 [8192, 1536], P(('dp', 'row'), 'col')
- grad_attn_gain: float32 [1536], P('col')
- grad_query: float32 [1536, 1536], P('col', 'row')
- grad_key: float32 [1536, 768], P('col', 'row')
- grad_value: float32 [1536, 768], P('col', 'row')
- grad_output: float32 [1536, 1536], P('row', 'col')
- grad_mlp_gain: float32 [1536], P('col')
- grad_gate: float32 [1536, 4096], P('col', 'row')
- grad_up: float32 [1536, 4096], P('col', 'row')
- grad_down: float32 [4096, 1536], P('row', 'col')
The draws below stay inside these ranges and needn't reach their ends.
All inputs are finite; a program needn't handle non-finite values.
Results may differ from the reference program's by a relative error of at most 0.018.
Values may be sent and summed in bfloat16 or wider, within the bound.
No kernel may reach another device: no remote copies, remote signals or barrier semaphores. Data moves between devices by JAX's collectives and lax.ppermute only.
A program may use at most 192 MiB of HBM per device.

```python
import jax
import jax.numpy as jnp
from jax import lax

D = 1536
HEADS = 16
KV_HEADS = 8
HEAD_DIM = 96
FF = 4096
SEQ_LEN = 1024
TOKENS = 8192


def shard_levels(key, shape, pieces, low, top_value):
    level = 1.0
    for dim, blocks in pieces:
        steps = jax.random.uniform(jax.random.fold_in(jax.random.fold_in(key, 6), dim), (blocks,), jnp.float32, low / len(pieces), top_value / len(pieces))
        level = level * jnp.repeat(jnp.exp(steps), shape[dim] // blocks).reshape((-1,) + (1,) * (len(shape) - 1 - dim))
    return level


def normal_values(own_key, dims, scale, most, cuts=(), kind=jnp.bfloat16):
    values = scale * jax.random.normal(own_key, dims, jnp.float32)
    if cuts:
        values = values * shard_levels(own_key, dims, cuts, -0.22, 0.18)
    return jnp.clip(values, -most, most).astype(kind)


def setup_inputs(seed: int = 0) -> dict:
    key_list = jax.random.split(jax.random.key(seed), 12)
    hidden_in = normal_values(key_list[0], (TOKENS, D), 1.0, 6.0, ((0, 16), (1, 2)))
    attn_gain = jnp.clip(1.0 + 0.1 * jax.random.normal(key_list[1], (D,), jnp.float32), 0.5, 1.5)
    w_query = normal_values(key_list[2], (D, HEADS * HEAD_DIM), D ** -0.5, 0.15625, ((0, 2), (1, 4)))
    w_key = normal_values(key_list[3], (D, KV_HEADS * HEAD_DIM), D ** -0.5, 0.15625, ((0, 2), (1, 4)))
    w_value = normal_values(key_list[4], (D, KV_HEADS * HEAD_DIM), D ** -0.5, 0.15625, ((0, 2), (1, 4)))
    w_output = normal_values(key_list[5], (HEADS * HEAD_DIM, D), (HEADS * HEAD_DIM // 64) ** -0.5, 1.25, ((0, 4), (1, 2)))
    mlp_gain = jnp.clip(1.0 + 0.1 * jax.random.normal(key_list[6], (D,), jnp.float32), 0.5, 1.5)
    w_gate = normal_values(key_list[7], (D, FF), D ** -0.5, 0.15625, ((0, 2), (1, 4)))
    w_up = normal_values(key_list[8], (D, FF), D ** -0.5, 0.15625, ((0, 2), (1, 4)))
    w_down = normal_values(key_list[9], (FF, D), FF ** -0.5, 0.09375, ((0, 4), (1, 2)))
    grad_out = normal_values(key_list[10], (TOKENS, D), 1.0, 6.0, ((0, 16), (1, 2)))
    return {"hidden_in": hidden_in, "attn_gain": attn_gain, "w_query": w_query, "w_key": w_key, "w_value": w_value, "w_output": w_output, "mlp_gain": mlp_gain, "w_gate": w_gate, "w_up": w_up, "w_down": w_down, "grad_out": grad_out}


EPSILON = 1e-05
ROPE_BASE = 100000.0
MASKED = -1e+30
PRECISE = lax.Precision.HIGHEST

@jax.custom_vjp
def low(v):
    return lax.optimization_barrier(v.astype(jnp.bfloat16)).astype(jnp.float32)

@jax.custom_vjp
def low_back(v):
    return v

def low_keep(v):
    return (low(v), None)

def low_pass(kept, grad):
    return (grad,)

def back_keep(v):
    return (v, None)

def back_low(kept, grad):
    return (low(grad),)
low.defvjp(low_keep, low_pass)
low_back.defvjp(back_keep, back_low)

def rms_scale(values, gain_vec):
    return values * lax.rsqrt(lax.optimization_barrier(jnp.mean(values * values, axis=-1, keepdims=True)) + EPSILON) * gain_vec

def matmul(left_mat, right_mat):
    return jnp.dot(left_mat, right_mat, precision=PRECISE)

def rope_tables(length):
    half_dim = HEAD_DIM // 2
    frequency = ROPE_BASE ** (-(jnp.arange(half_dim).astype(jnp.float32) * 2.0) / HEAD_DIM)
    angles = jnp.arange(length).astype(jnp.float32)[:, None] * frequency[None, :]
    return (jnp.cos(angles), jnp.sin(angles))

def rotate(values, cosine, sine_val):
    half_dim = values.shape[-1] // 2
    first_half = values[..., :half_dim]
    second_half = values[..., half_dim:]
    cos_b = cosine[:, None, :]
    sin_b = sine_val[:, None, :]
    return jnp.concatenate([first_half * cos_b - second_half * sin_b, second_half * cos_b + first_half * sin_b], axis=-1)

def layer_forward(hidden_in, attn_gain, w_query, w_key, w_value, w_output, mlp_gain, w_gate, w_up, w_down):
    length = hidden_in.shape[0]
    groups = HEADS // KV_HEADS
    cosine, sine_val = rope_tables(length)
    normed = low(rms_scale(hidden_in, attn_gain))
    proj_q = low_back(matmul(normed, w_query))
    proj_k = low_back(matmul(normed, w_key))
    proj_v = low_back(matmul(normed, w_value))
    queries = low(rotate(proj_q.reshape(length, HEADS, HEAD_DIM), cosine, sine_val)).reshape(length, KV_HEADS, groups, HEAD_DIM)
    key_rows = low(rotate(proj_k.reshape(length, KV_HEADS, HEAD_DIM), cosine, sine_val))
    value_rows = low(proj_v).reshape(length, KV_HEADS, HEAD_DIM)
    scores = low_back(jnp.einsum('qkgd,lkd->kgql', queries, key_rows, precision=PRECISE) * HEAD_DIM ** (-0.5))
    causal = jnp.arange(length)[None, :] <= jnp.arange(length)[:, None]
    scores = jnp.where(causal, scores, MASKED)
    row_max = lax.optimization_barrier(jnp.max(scores, axis=-1, keepdims=True))
    expo = jnp.exp(scores - row_max)
    attn_probs = low(expo / lax.optimization_barrier(jnp.sum(expo, axis=-1, keepdims=True)))
    mixed_heads = jnp.einsum('kgql,lkd->qkgd', attn_probs, value_rows, precision=PRECISE).reshape(length, HEADS * HEAD_DIM)
    mixed_heads = low_back(low(mixed_heads))
    attn_out = low_back(matmul(mixed_heads, w_output))
    middle = hidden_in + attn_out
    normed_two = low(rms_scale(middle, mlp_gain))
    gate_val = low_back(matmul(normed_two, w_gate))
    up_val = low_back(matmul(normed_two, w_up))
    hidden_act = low(jax.nn.silu(gate_val) * up_val)
    return middle + low_back(matmul(hidden_act, w_down))

def reference(hidden_in, attn_gain, w_query, w_key, w_value, w_output, mlp_gain, w_gate, w_up, w_down, grad_out):
    params = tuple((array_in.astype(jnp.float32) for array_in in (attn_gain, w_query, w_key, w_value, w_output, mlp_gain, w_gate, w_up, w_down)))
    seq_total = hidden_in.shape[0] // SEQ_LEN
    inputs = hidden_in.astype(jnp.float32).reshape(seq_total, SEQ_LEN, D)
    cotangents = grad_out.astype(jnp.float32).reshape(seq_total, SEQ_LEN, D)

    def one_sequence(running, seq_pair):
        seq_in, seq_grad = seq_pair
        result, pullback = jax.vjp(layer_forward, seq_in, *params)
        seq_grads = pullback(seq_grad)
        running = tuple((total_val + grad_val for total_val, grad_val in zip(running, seq_grads[1:])))
        return (running, (result, seq_grads[0]))
    zero_grads = tuple((jnp.zeros_like(param_val) for param_val in params))
    totals, (outputs, grad_rows) = lax.scan(one_sequence, zero_grads, (inputs, cotangents))
    return (outputs.reshape(seq_total * SEQ_LEN, D).astype(jnp.bfloat16), grad_rows.reshape(seq_total * SEQ_LEN, D), totals[0], totals[1], totals[2], totals[3], totals[4], totals[5], totals[6], totals[7], totals[8])
```

```python
import functools

import jax
import jax.numpy as jnp
from jax import lax
from jax.experimental import pallas as pl
from jax.experimental.pallas import tpu as pltpu
from jax.sharding import PartitionSpec as P

HEAD_DIM = 96
SEQ_LEN = 1024
EPSILON = 1e-05
ROPE_BASE = 100000.0
MASKED = -1e30
BF = jnp.bfloat16
F32 = jnp.float32
SCALE = HEAD_DIM ** (-0.5)


NT = (((1,), (1,)), ((), ()))
TN = (((0,), (0,)), ((), ()))


def mm(left_mat, right_mat):
    return jnp.dot(left_mat, right_mat, preferred_element_type=F32)


def mm_nt(left_mat, right_mat):
    return lax.dot_general(left_mat, right_mat, NT, preferred_element_type=F32)


def mm_tn(left_mat, right_mat):
    return lax.dot_general(left_mat, right_mat, TN, preferred_element_type=F32)


def attend_forward_kernel(
    own_ref, ha_ref, hb_ref, gain_ref, w0_ref, w1_ref, cos_ref, sin_ref,
    normed_ref, mixed_ref, q_ref, k_ref, v_ref, lse_ref, vt_ref, ot_ref,
):
    own = own_ref[0]
    heads, length, _ = q_ref.shape
    kv_heads = k_ref.shape[0]
    groups = heads // kv_heads
    quarter = length // 4
    half_width = w0_ref.shape[0]
    half_dim = HEAD_DIM // 2
    gain_row = gain_ref[...]
    for place in range(4):
        source = ha_ref if place < 2 else hb_ref
        start = (place % 2) * quarter
        hidden = source[start : start + quarter, :].astype(F32)
        mean_sq = jnp.sum(hidden * hidden, axis=1, keepdims=True) / (2 * half_width)
        normed = (hidden * lax.rsqrt(mean_sq + EPSILON) * gain_row).astype(BF)
        normed_ref[place * quarter : (place + 1) * quarter, :] = normed
        proj = mm(normed[:, :half_width], w0_ref[...]) + mm(normed[:, half_width:], w1_ref[...])
        rows = pl.ds(pl.multiple_of(jnp.bitwise_xor(own, place) * quarter, quarter), quarter)
        cosine = cos_ref[rows, :]
        sine = sin_ref[rows, :]
        for head in range(heads + kv_heads):
            part = proj[:, head * HEAD_DIM : (head + 1) * HEAD_DIM]
            swapped = jnp.concatenate([part[:, half_dim:], part[:, :half_dim]], axis=1)
            rotated = (part * cosine + swapped * sine).astype(BF)
            if head < heads:
                q_ref[head, rows, :] = rotated
            else:
                k_ref[head - heads, rows, :] = rotated
        for head in range(kv_heads):
            col = (heads + kv_heads + head) * HEAD_DIM
            v_ref[head, rows, :] = proj[:, col : col + HEAD_DIM].astype(BF)
    for head in range(kv_heads):
        vt_ref[head, :, :] = v_ref[head, :, :].T
    for block in range(4):
        span = (block + 1) * quarter

        def one_head(head, carry):
            kv = head // groups
            block_q = q_ref[head, block * quarter : span, :]
            scores = mm_nt(k_ref[kv, :span, :], block_q) * SCALE
            key_pos = lax.broadcasted_iota(jnp.int32, (span, quarter), 0)
            query_pos = lax.broadcasted_iota(jnp.int32, (span, quarter), 1) + block * quarter
            scores = jnp.where(key_pos <= query_pos, scores, MASKED)
            row_max = jnp.max(scores, axis=0, keepdims=True)
            expo = jnp.exp(scores - row_max)
            total = jnp.sum(expo, axis=0, keepdims=True)
            probs = (expo * (1.0 / total)).astype(BF)
            ot_ref[head, :, :] = mm(vt_ref[kv, :, :span], probs)
            lse_ref[head, block, :, :] = row_max + jnp.log(total)
            return carry

        lax.fori_loop(0, heads, one_head, 0)
        rows = pl.ds(pl.multiple_of(jnp.bitwise_xor(own, block) * quarter, quarter), quarter)
        mixed_ref[rows, :] = jnp.concatenate(
            [ot_ref[head].T for head in range(heads)], axis=1
        ).astype(BF)


def attend_forward(own, half_a, half_b, gain, w0, w1, cosine, sine, heads, kv_heads):
    length = half_a.shape[0] * 2
    width = half_a.shape[1]
    shapes = (
        jax.ShapeDtypeStruct((length, width), BF),
        jax.ShapeDtypeStruct((length, heads * HEAD_DIM), BF),
        jax.ShapeDtypeStruct((heads, length, HEAD_DIM), BF),
        jax.ShapeDtypeStruct((kv_heads, length, HEAD_DIM), BF),
        jax.ShapeDtypeStruct((kv_heads, length, HEAD_DIM), BF),
        jax.ShapeDtypeStruct((heads, 4, 1, length // 4), F32),
    )
    return pl.pallas_call(
        attend_forward_kernel,
        out_shape=shapes,
        in_specs=[pl.BlockSpec(memory_space=pltpu.SMEM)]
        + [pl.BlockSpec(memory_space=pltpu.VMEM)] * 7,
        out_specs=tuple(pl.BlockSpec(memory_space=pltpu.VMEM) for _ in shapes),
        scratch_shapes=[
            pltpu.VMEM((kv_heads, HEAD_DIM, length), BF),
            pltpu.VMEM((heads, HEAD_DIM, length // 4), F32),
        ],
        compiler_params=pltpu.CompilerParams(vmem_limit_bytes=56 * 2**20),
        name="attend_forward",
    )(own, half_a, half_b, gain, w0, w1, cosine, sine)


def attend_back_kernel(
    own_ref, ga_ref, gb_ref, wo0_ref, wo1_ref, q_ref, k_ref, v_ref, lse_ref, cos_ref, sin_ref,
    out_ref, gm_ref, kt_ref, dq_ref, dk_ref, dv_ref,
):
    own = own_ref[0]
    heads, length, _ = q_ref.shape
    kv_heads = k_ref.shape[0]
    groups = heads // kv_heads
    quarter = length // 4
    half_width = wo0_ref.shape[1]
    half_dim = HEAD_DIM // 2
    for place in range(4):
        source = ga_ref if place < 2 else gb_ref
        start = (place % 2) * quarter
        grad = source[start : start + quarter, :]
        grad_mixed = (
            mm_nt(grad[:, :half_width], wo0_ref[...]) + mm_nt(grad[:, half_width:], wo1_ref[...])
        ).astype(BF)
        rows = pl.ds(pl.multiple_of(jnp.bitwise_xor(own, place) * quarter, quarter), quarter)
        for head in range(heads):
            gm_ref[head, rows, :] = grad_mixed[:, head * HEAD_DIM : (head + 1) * HEAD_DIM]
    for head in range(kv_heads):
        kt_ref[head, :, :] = k_ref[head, :, :].T
    dk_ref[...] = jnp.zeros(dk_ref.shape, F32)
    dv_ref[...] = jnp.zeros(dv_ref.shape, F32)
    for block in range(4):
        span = (block + 1) * quarter

        def one_head(head, carry):
            kv = head // groups
            block_q = q_ref[head, block * quarter : span, :]
            block_grad = gm_ref[head, block * quarter : span, :]
            scores = mm_nt(k_ref[kv, :span, :], block_q) * SCALE
            key_pos = lax.broadcasted_iota(jnp.int32, (span, quarter), 0)
            query_pos = lax.broadcasted_iota(jnp.int32, (span, quarter), 1) + block * quarter
            scores = jnp.where(key_pos <= query_pos, scores, MASKED)
            probs = jnp.exp(scores - lse_ref[head, block, :, :])
            grad_probs = mm_nt(v_ref[kv, :span, :], block_grad)
            inner = jnp.sum(grad_probs * probs, axis=0, keepdims=True)
            grad_scores = (probs * (grad_probs - inner)).astype(BF)
            dq_ref[head, block, :, :] = mm(kt_ref[kv, :, :span], grad_scores) * SCALE
            dk_ref[kv, :span, :] += mm(grad_scores, block_q) * SCALE
            dv_ref[kv, :span, :] += mm(probs.astype(BF), block_grad)
            return carry

        lax.fori_loop(0, heads, one_head, 0)
    for place in range(4):
        true_place = jnp.bitwise_xor(own, place)
        rows = pl.ds(pl.multiple_of(true_place * quarter, quarter), quarter)
        cosine = cos_ref[rows, :]
        sine = sin_ref[rows, :]
        pieces = []
        for head in range(heads + kv_heads):
            if head < heads:
                part = dq_ref[head, true_place, :, :].T
            else:
                part = dk_ref[head - heads, rows, :]
            swapped = jnp.concatenate([part[:, half_dim:], part[:, :half_dim]], axis=1)
            pieces.append(part * cosine - swapped * sine)
        for head in range(kv_heads):
            pieces.append(dv_ref[head, rows, :])
        out_ref[place * quarter : (place + 1) * quarter, :] = jnp.concatenate(
            pieces, axis=1
        ).astype(BF)


def attend_back(own, grad_a, grad_b, wo0, wo1, queries, key_rows, value_rows, lse, cosine, sine):
    heads, length, _ = queries.shape
    kv_heads = key_rows.shape[0]
    return pl.pallas_call(
        attend_back_kernel,
        out_shape=jax.ShapeDtypeStruct((length, (heads + 2 * kv_heads) * HEAD_DIM), BF),
        in_specs=[pl.BlockSpec(memory_space=pltpu.SMEM)]
        + [pl.BlockSpec(memory_space=pltpu.VMEM)] * 10,
        out_specs=pl.BlockSpec(memory_space=pltpu.VMEM),
        scratch_shapes=[
            pltpu.VMEM((heads, length, HEAD_DIM), BF),
            pltpu.VMEM((kv_heads, HEAD_DIM, length), BF),
            pltpu.VMEM((heads, 4, HEAD_DIM, length // 4), F32),
            pltpu.VMEM((kv_heads, length, HEAD_DIM), F32),
            pltpu.VMEM((kv_heads, length, HEAD_DIM), F32),
        ],
        compiler_params=pltpu.CompilerParams(vmem_limit_bytes=56 * 2**20),
        name="attend_back",
    )(own, grad_a, grad_b, wo0, wo1, queries, key_rows, value_rows, lse, cosine, sine)


X_SWAP = [(0, 2), (1, 3), (2, 0), (3, 1)]
CORE_SWAP = [(0, 1), (1, 0), (2, 3), (3, 2)]
COL_SWAP = [(0, 1), (1, 0)]


def flat_place(x_place, core, col):
    return (x_place * 2 + core) * 2 + col


def ring_pairs(backward):
    pairs = []
    for x_place in range(2):
        for core in range(2):
            for col in range(2):
                turn = (x_place == col) != backward
                target = (1 - x_place, col) if turn else (x_place, 1 - col)
                pairs.append(
                    (flat_place(x_place, core, col), flat_place(target[0], core, target[1]))
                )
    return pairs


def cross_pairs():
    pairs = []
    for core in range(2):
        for x_place in range(2):
            col = 1 - x_place
            pairs.append(
                (flat_place(x_place, core, col), flat_place(1 - x_place, core, 1 - col))
            )
    return pairs


def x_swap(values):
    return lax.ppermute(values, "row", X_SWAP)


def core_swap(values):
    return lax.ppermute(values, "row", CORE_SWAP)


def col_swap(values):
    return lax.ppermute(values, "col", COL_SWAP)


def spread_in(block, straight, x_place):
    quarter = block.shape[0] // 2
    ring = lax.ppermute(block, ("row", "col"), ring_pairs(False))
    cross = lax.ppermute(block, ("row", "col"), cross_pairs())
    joined = jnp.concatenate(
        [jnp.where(straight, block, ring), jnp.where(straight, ring, cross)], axis=1
    )
    first = joined[:quarter]
    second = joined[quarter:]
    flip = x_place == 1
    half_a = jnp.concatenate(
        [jnp.where(flip, second, first), jnp.where(flip, first, second)], axis=0
    )
    return half_a, core_swap(half_a)


def spread_out(values, straight, x_place):
    half_width = values.shape[1] // 2
    low = values.astype(BF)
    keep = low[:, :half_width]
    give = low[:, half_width:]
    ring = lax.ppermute(jnp.where(straight, give, keep), ("row", "col"), ring_pairs(True))
    cross = lax.ppermute(give, ("row", "col"), cross_pairs())
    mine = jnp.where(straight, values[:, :half_width], ring.astype(F32))
    other = jnp.where(straight, ring, cross).astype(F32)
    flip = x_place == 1
    return jnp.concatenate([jnp.where(flip, other, mine), jnp.where(flip, mine, other)], axis=0)


def gather_group(values):
    half_a = jnp.concatenate([values, x_swap(values)], axis=0)
    return half_a, core_swap(half_a)


def scatter_group(partial):
    half = partial.shape[0] // 2
    quarter = half // 2
    received = core_swap(partial[half:])
    chip_sum = partial[:half].astype(F32) + received.astype(F32)
    far = x_swap(chip_sum[quarter:].astype(BF))
    return chip_sum[:quarter] + far.astype(F32)


def inverse_rms(values):
    return lax.rsqrt(jnp.mean(values * values, axis=1, keepdims=True) + EPSILON)


def norm_back(values, inv_rms, gain_row, grad_normed):
    scaled = grad_normed * gain_row
    row_dots = jnp.mean(scaled * values, axis=1, keepdims=True)
    grad_values = scaled * inv_rms - values * (inv_rms**3 * row_dots)
    grad_gain = jnp.sum(grad_normed * values * inv_rms, axis=0)
    return grad_values, grad_gain


def rope_tables():
    half_dim = HEAD_DIM // 2
    frequency = ROPE_BASE ** (-(jnp.arange(half_dim).astype(F32) * 2.0) / HEAD_DIM)
    angles = jnp.arange(SEQ_LEN).astype(F32)[:, None] * frequency[None, :]
    cosine = jnp.cos(angles)
    sine = jnp.sin(angles)
    return (
        jnp.concatenate([cosine, cosine], axis=1),
        jnp.concatenate([-sine, sine], axis=1),
    )


def share_grad(left_mat, right_mat, width_side):
    if width_side == 0:
        half = left_mat.shape[1] // 2
        mine = mm_tn(left_mat[:, :half], right_mat)
        other = mm_tn(left_mat[:, half:], right_mat)
    else:
        half = right_mat.shape[1] // 2
        mine = mm_tn(left_mat, right_mat[:, :half])
        other = mm_tn(left_mat, right_mat[:, half:])
    return (mine + col_swap(other.astype(BF)).astype(F32)).astype(BF)


def per_device(
    hidden_in, attn_gain, w_query, w_key, w_value, w_output, mlp_gain, w_gate, w_up, w_down,
    grad_out,
):
    row = lax.axis_index("row")
    col = lax.axis_index("col")
    x_place = row // 2
    core = row % 2
    straight = x_place == col
    own = jnp.reshape(core * 2 + x_place, (1,)).astype(jnp.int32)
    heads = w_query.shape[1] // HEAD_DIM
    kv_heads = w_key.shape[1] // HEAD_DIM
    q_width = w_query.shape[1]
    k_width = w_key.shape[1]
    ff_width = w_gate.shape[1]

    ha, hb = spread_in(hidden_in, straight, x_place)
    w_in0 = jnp.concatenate([w_query, w_key, w_value], axis=1)
    w_in1 = col_swap(w_in0)
    gains0 = jnp.stack([attn_gain, mlp_gain])
    gains = jnp.concatenate([gains0, col_swap(gains0)], axis=1)
    wo0 = w_output
    wo1 = col_swap(w_output)
    wd1 = col_swap(w_down)
    ga, gb = spread_in(grad_out, straight, x_place)
    wg1 = col_swap(w_gate)
    wu1 = col_swap(w_up)
    cosine, sine = rope_tables()

    normed, mixed, queries, key_rows, value_rows, lse = attend_forward(
        own, ha, hb, gains[0:1], w_in0, w_in1, cosine, sine, heads, kv_heads
    )
    quarter = ha.shape[0] // 2
    hidden_own = ha[:quarter].astype(F32)
    wo = jnp.concatenate([wo0, wo1], axis=1)
    attn_out = scatter_group(mm(mixed, wo).astype(BF))
    middle = hidden_own + attn_out
    second_rms = inverse_rms(middle)
    gain_two = gains[1:2]
    normed_two = (middle * second_rms * gain_two).astype(BF)
    n2 = jnp.concatenate(gather_group(normed_two), axis=0)
    grad_all = jnp.concatenate([ga, gb], axis=0)
    wd = jnp.concatenate([w_down, wd1], axis=1)
    wg = jnp.concatenate([w_gate, wg1], axis=0)
    wu = jnp.concatenate([w_up, wu1], axis=0)
    grad_hidden = mm_nt(grad_all, wd)
    gate_val = mm(n2, wg)
    up_val = mm(n2, wu)
    sigmoid_val = jax.nn.sigmoid(gate_val)
    silu_val = gate_val * sigmoid_val
    hidden_act = (silu_val * up_val).astype(BF)
    grad_gate_val = (
        grad_hidden * up_val * sigmoid_val * (1.0 + gate_val * (1.0 - sigmoid_val))
    ).astype(BF)
    grad_up_val = (grad_hidden * silu_val).astype(BF)
    grad_n2 = scatter_group((mm_nt(grad_gate_val, wg) + mm_nt(grad_up_val, wu)).astype(BF))
    mlp_out = scatter_group(mm(hidden_act, wd).astype(BF))
    layer_out = spread_out(middle + mlp_out, straight, x_place).astype(BF)
    grad_mid_norm, grad_mlp_gain = norm_back(middle, second_rms, gain_two, grad_n2)
    grad_middle = ga[:quarter].astype(F32) + grad_mid_norm
    gma, gmb = gather_group(grad_middle.astype(BF))
    grad_proj = attend_back(
        own, gma, gmb, wo0, wo1, queries, key_rows, value_rows, lse, cosine, sine
    )
    w_in = jnp.concatenate([w_in0, w_in1], axis=0)
    grad_n1 = scatter_group(mm_nt(grad_proj, w_in).astype(BF))
    grad_in_norm, grad_attn_gain = norm_back(
        hidden_own, inverse_rms(hidden_own), gains[0:1], grad_n1
    )
    grad_in = spread_out(grad_middle + grad_in_norm, straight, x_place)

    def all_groups(grad):
        return lax.psum(grad, "dp").astype(F32)

    grad_down = all_groups(share_grad(hidden_act, grad_all, 1))
    grad_gate = all_groups(share_grad(n2, grad_gate_val, 0))
    grad_up = all_groups(share_grad(n2, grad_up_val, 0))
    grad_middle_rows = jnp.concatenate([gma, gmb], axis=0)
    grad_output = all_groups(share_grad(mixed, grad_middle_rows, 1))
    grad_inner = all_groups(share_grad(normed, grad_proj, 0))

    half = gains0.shape[1]
    gain_grads = jnp.stack([grad_attn_gain, grad_mlp_gain])
    gain_grads = gain_grads[:, :half] + col_swap(gain_grads[:, half:])
    gain_grads = lax.psum(gain_grads, ("dp", "row"))
    return (
        layer_out,
        grad_in,
        gain_grads[0],
        grad_inner[:, :q_width],
        grad_inner[:, q_width : q_width + k_width],
        grad_inner[:, q_width + k_width :],
        grad_output,
        gain_grads[1],
        grad_gate,
        grad_up,
        grad_down,
    )


def solution(mesh):
    tokens = P(("dp", "row"), "col")
    wide = P("col", "row")
    tall = P("row", "col")
    gain = P("col")
    return jax.shard_map(
        per_device,
        mesh=mesh,
        in_specs=(tokens, gain, wide, wide, wide, tall, gain, wide, wide, tall, tokens),
        out_specs=(tokens, tokens, gain, wide, wide, wide, tall, gain, wide, wide, tall),
        check_vma=False,
    )
```
